256 devices in a mesh: head: 16 (over z, core), tail: 16 (over y, x).
Axes of the slice: x: 4, y: 4, z: 8, core: 2. Of those that a mesh axis runs over, the one named last changes fastest.
Arguments:
- head_emb: bfloat16 [131072, 800], P(('head', 'tail')), may hold values from -48 to 48
- head_state: float32 [131072], P(('head', 'tail')), may hold values from 0.01 to 1
- tail_emb: bfloat16 [64, 128, 800], P('tail'), may hold values from -1.5 to 1.5
- tail_state: float32 [64, 128], P('tail'), may hold values from 0.01 to 1
- relation_emb: bfloat16 [1024, 800], replicated, may hold values from -3.5 to 3.5
- head_rows: int32 [1024, 256], P(('head', 'tail')), may hold values from 0 to 511
- relations: int32 [1024, 256], P(('head', 'tail')), may hold values from 0 to 1023
- tail_offsets: int32 [1024, 256], P(('head', 'tail')), may hold values from 0 to 127
- tail_owner: int32 [1024, 1], P(('head', 'tail')), may hold values from 0 to 15; in each aligned block of 4 rows (0 to 3, 4 to 7, ...) at most 2 rows name the same one
- tail_local: int32 [1024], P(('head', 'tail')), may hold values from 0 to 3
- block_count: int32 [256], P(('head', 'tail')), may hold values from 1 to 4, as said below
- neg_blocks: int32 [8], replicated, may hold values from 0 to 63, as said below
Outputs:
- head_new: bfloat16 [131072, 800], P(('head', 'tail'))
- head_state_new: float32 [131072], P(('head', 'tail'))
- tail_new: bfloat16 [64, 128, 800], P('tail')
- tail_state_new: float32 [64, 128], P('tail')
The draws below stay inside these ranges and needn't reach their ends.
Inputs may be any that keep to these rules, and one draw needn't show every extreme that they name: `tail_owner`: no tail index owns the tail blocks of more than 2 edge block slots of one device, and in some devices one owns exactly 2. `block_count`: some device has all 4 slots live. `neg_blocks`: distinct tail blocks; the last tail block is always among them.
All inputs are finite; a program needn't handle non-finite values.
Results may differ from the reference program's by a relative error of at most 0.0012.
The reference program's roundings to bfloat16 on the way (of `negatives`, `query`, `neg_grad` and `block_grad`) count: a program that leaves them out, or rounds other values in their place, can miss the bound.
Values may be sent and summed in bfloat16 or wider, within the bound.
A program may use at most 128 MiB of HBM per device.

```python
import math
import jax
import jax.numpy as jnp
import numpy as np
from jax import lax

EDGES = 256
TBS = 128
NEGB = 8
RELS = 1024
HROWS = 512
TB_DEV = 4
EB_DEV = 4
WIDTH = 800
NEG = 1024
DEVS = 256
CAP = 2
HEADS = 131072
TBLOCKS = 64
EBLOCKS = 1024
N_HEAD = 16
N_TAIL = 16


def draw_head_emb(key, part):
    values_drawn = jnp.clip(jax.random.normal(key, (HEADS, WIDTH), jnp.float32), -6.0, 6.0) * 0.25
    row_ids = jnp.arange(HEADS, dtype=jnp.int32)
    spiked_start = N_HEAD // 2 * N_TAIL * HROWS
    in_spike = (row_ids >= spiked_start) & (row_ids < spiked_start + N_TAIL * HROWS)
    values_drawn = values_drawn * jnp.where(in_spike, 32.0, 1.0)[:, None]
    values_drawn = jnp.clip(values_drawn, -48.0, 48.0)
    return values_drawn.astype(jnp.bfloat16)


def draw_block_count(key, part):
    halvings = jax.random.randint(key, (DEVS,), 0, 4)
    counts = jnp.maximum(EB_DEV // jnp.left_shift(jnp.ones((DEVS,), jnp.int32), halvings), 1)
    return counts.at[0].set(EB_DEV).astype(jnp.int32)


def draw_neg_blocks(key, part):
    others = jax.random.permutation(key, TBLOCKS - 1)[:NEGB - 1].astype(jnp.int32)
    chosen = jnp.concatenate([others, jnp.full((1,), TBLOCKS - 1, jnp.int32)])
    turn = jax.random.randint(jax.random.fold_in(key, 3), (), 0, NEGB)
    return jnp.roll(chosen, turn).astype(jnp.int32)


def with_ends(result, stream_key, low, top_value):
    longest = result.shape.index(max(result.shape))
    spots = []
    for shift in (0, 1):
        where = [jax.random.randint(jax.random.fold_in(stream_key, axis), (), 0, length) for axis, length in enumerate(result.shape)]
        where[longest] = (where[longest] + shift) % result.shape[longest]
        spots.append(tuple(where))
    return result.at[spots[0]].set(low).at[spots[1]].set(top_value)


def shard_levels(rng, dims, shards, low, high):
    def one(axis_at, parts):
        draws = jax.random.uniform(jax.random.fold_in(jax.random.fold_in(rng, 6), axis_at), (parts,), jnp.float32, low / len(shards), high / len(shards))
        return jnp.repeat(jnp.exp(draws), dims[axis_at] // parts).reshape((-1,) + (1,) * (len(dims) - axis_at - 1))

    factor_of = one(*shards[0])
    for cut in shards[1:]:
        factor_of = factor_of * one(*cut)
    return factor_of


def cumulative_ranks(number_of, skew):
    weights = [(1 << 20) // math.isqrt(rank ** skew) + 1 for rank in range(1, number_of + 1)]
    spread = 1 + sum(weights) // (1 << 30)
    return np.cumsum(np.array([max(1, weight // spread) for weight in weights]))


def skewed_ids(key, extent, amount, slope):
    grid = cumulative_ranks(amount, slope)
    lot = jax.random.randint(jax.random.fold_in(key, 1), extent, 0, int(grid[amount - 1]))
    standing = jnp.searchsorted(jnp.asarray(grid, jnp.int32), lot, side="right")
    return jax.random.permutation(jax.random.fold_in(key, 2), amount)[standing].astype(jnp.int32)


def deal_out(rng, own, number, rows, number_of, top, limit, skew):
    ranking = jax.random.permutation(rng, number_of)
    crowded, ordinary = portions_of(number_of, rows * top, limit, skew, True), portions_of(number_of, rows * top, limit, skew, False)
    places = jnp.arange(number_of)

    def named(lengths, rotation):
        used = int((lengths > 0).sum())
        fixed = max(1, used // 4)
        moved = fixed + (places - fixed + rotation * (used - fixed)) % max(1, number_of - fixed)
        return jnp.zeros((number_of,), jnp.int32).at[ranking[jnp.where(places < fixed, places, moved)]].set(jnp.asarray(lengths, jnp.int32))

    lengths = jnp.where(number % 4 == 0, named(crowded, number // 4), named(ordinary, number - number // 4 - 1))
    mixed = jax.random.permutation(jax.random.fold_in(own, 3), number_of)
    source_of, taker = mixed[0:number_of // 2 * 2:2], mixed[1:number_of // 2 * 2:2]
    room = jnp.minimum(lengths[source_of] - 1, limit - lengths[taker]) // 2
    room = jnp.where((source_of == ranking[0]) | (taker == ranking[0]) | (lengths[taker] == 0), 0, jnp.maximum(room, 0))
    moved = jax.random.randint(jax.random.fold_in(own, 4), (number_of // 2,), 0, 1 << 20) % (room + 1)
    lengths = lengths.at[source_of].add(-moved).at[taker].add(moved)
    members = jnp.searchsorted(jnp.cumsum(lengths), jnp.arange(rows * top), side="right").astype(jnp.int32)
    grid = members.reshape(top, rows).T
    grid = grid[jax.random.permutation(jax.random.fold_in(own, 1), rows)]
    rotation = jax.random.randint(jax.random.fold_in(own, 2), (rows, 1), 0, top)
    return jnp.take_along_axis(grid, (jnp.arange(top)[None, :] + rotation) % top, axis=1)


def portions_of(amount, total, limit, lean, full):
    weights = [(1 << 20) // math.isqrt(standing ** lean) + 1 for standing in range(1, amount + 1)]
    largest = limit if full else min(limit, max(-(-total // amount), total * weights[0] // sum(weights)))
    least = 1 if total - largest >= amount - 1 else 0
    holding, surplus = [largest] + [least] * (amount - 1), total - largest - least * (amount - 1)
    while surplus > 0:
        free = [i for i in range(1, amount) if holding[i] < largest] or [i for i in range(1, amount) if holding[i] < limit]
        whole, left = sum([weights[i] for i in free]), surplus
        for i in free:
            extra = min(limit - holding[i], max(1, left * weights[i] // whole), surplus)
            holding[i] = holding[i] + extra
            surplus = surplus - extra
    return np.array(holding)


def gaussian(key, shape, scale, limit, pieces=(), held_as=jnp.bfloat16):
    array = jax.random.normal(key, shape, jnp.float32) * scale
    if len(pieces) > 0:
        array = shard_levels(key, shape, pieces, -0.22, 0.18) * array
    return jnp.clip(array, min=-limit, max=limit).astype(held_as)


def setup_inputs(seed: int = 0) -> dict:
    key_list = jax.random.split(jax.random.key(seed), 13)
    head_emb = draw_head_emb(jax.random.fold_in(key_list[12], 71), 0)
    head_state = jnp.clip(jnp.exp(math.log(1.0) - 4.6051702 * jax.random.uniform(key_list[1], (HEADS,), jnp.float32) ** shard_levels(key_list[1], (HEADS,), ((0, 256),), -0.2, 0.2)), 0.01, 1.0)
    tail_emb = gaussian(key_list[2], (TBLOCKS, TBS, WIDTH), 0.25, 1.5, ((0, 16),))
    tail_state = jnp.clip(jnp.exp(math.log(1.0) - 4.6051702 * jax.random.uniform(key_list[3], (TBLOCKS, TBS), jnp.float32) ** shard_levels(key_list[3], (TBLOCKS, TBS), ((0, 16),), -0.2, 0.2)), 0.01, 1.0)
    relation_emb = gaussian(key_list[4], (RELS, WIDTH), 0.7, 3.5)
    head_rows = with_ends(jax.random.randint(key_list[5], (EBLOCKS, EDGES), 0, HROWS), jax.random.fold_in(key_list[5], 1), 0, HROWS - 1).astype(jnp.int32)
    relations = with_ends(skewed_ids(key_list[6], (EBLOCKS, EDGES), RELS, 2), jax.random.fold_in(key_list[6], 3), 0, RELS - 1).astype(jnp.int32)
    tail_offsets = with_ends(jax.random.randint(key_list[7], (EBLOCKS, EDGES), 0, TBS), jax.random.fold_in(key_list[7], 1), 0, TBS - 1).astype(jnp.int32)
    tail_owner_keys = jax.random.split(jax.random.fold_in(key_list[8], 1), EBLOCKS // EB_DEV)
    tail_owner_turns = jax.random.permutation(jax.random.fold_in(key_list[8], 3), EBLOCKS // EB_DEV)
    tail_owner = jax.vmap(lambda own, number: deal_out(jax.random.fold_in(key_list[8], 2), own, number, EB_DEV, N_TAIL, 1, CAP, 2))(tail_owner_keys, tail_owner_turns).reshape((EBLOCKS, 1))
    tail_local = with_ends(jax.random.randint(key_list[9], (EBLOCKS,), 0, TB_DEV), jax.random.fold_in(key_list[9], 1), 0, TB_DEV - 1).astype(jnp.int32)
    block_count = draw_block_count(jax.random.fold_in(key_list[12], 71), 0)
    neg_blocks = draw_neg_blocks(jax.random.fold_in(key_list[12], 71), 0)
    return {"head_emb": head_emb, "head_state": head_state, "tail_emb": tail_emb, "tail_state": tail_state, "relation_emb": relation_emb, "head_rows": head_rows, "relations": relations, "tail_offsets": tail_offsets, "tail_owner": tail_owner, "tail_local": tail_local, "block_count": block_count, "neg_blocks": neg_blocks}


LEARN_RATE = 0.3

def complex_product(left, right):
    half_width = left.shape[-1] // 2
    left_re, left_im = (left[..., :half_width], left[..., half_width:])
    right_re, right_im = (right[..., :half_width], right[..., half_width:])
    return jnp.concatenate([left_re * right_re - left_im * right_im, left_re * right_im + left_im * right_re], axis=-1)

def conj_product(left, right):
    half_width = left.shape[-1] // 2
    left_re, left_im = (left[..., :half_width], left[..., half_width:])
    right_re, right_im = (right[..., :half_width], right[..., half_width:])
    return jnp.concatenate([left_re * right_re + left_im * right_im, left_im * right_re - left_re * right_im], axis=-1)

def row_adagrad(embedding, adagrad_state, gradient):
    state_next = adagrad_state + lax.optimization_barrier(jnp.mean(gradient * gradient, axis=-1))
    updated = embedding.astype(jnp.float32) - LEARN_RATE * gradient / jnp.sqrt(state_next)[..., None]
    return (updated.astype(jnp.bfloat16), state_next)

def reference(head_emb, head_state, tail_emb, tail_state, relation_emb, head_rows, relations, tail_offsets, tail_owner, tail_local, block_count, neg_blocks):
    negatives = tail_emb[neg_blocks].reshape(NEG, WIDTH).astype(jnp.float32)
    global_block = (tail_owner[:, 0] * TB_DEV + tail_local).astype(jnp.int32).reshape(DEVS, EB_DEV)
    per_device = (head_emb.reshape(DEVS, HROWS, WIDTH), head_state.reshape(DEVS, HROWS), head_rows.reshape(DEVS, EB_DEV, EDGES), relations.reshape(DEVS, EB_DEV, EDGES), tail_offsets.reshape(DEVS, EB_DEV, EDGES), global_block, block_count)

    def one_device(totals, device_item):
        grad_table, neg_total = totals
        embedding, adagrad_state, row_ids, relation_ids, offset_ids, block_ids, live_count = device_item
        live_mask = jnp.repeat((jnp.arange(EB_DEV, dtype=jnp.int32) < live_count).astype(jnp.float32), EDGES)
        chosen = tail_emb[block_ids].reshape(EB_DEV * TBS, WIDTH)
        tail_index = (jnp.arange(EB_DEV, dtype=jnp.int32)[:, None] * TBS + offset_ids).reshape(-1).astype(jnp.int32)
        flat_rows = row_ids.reshape(-1).astype(jnp.int32)
        tail_vectors = chosen[tail_index].astype(jnp.float32)
        head_vectors = embedding[flat_rows].astype(jnp.float32)
        relation_vectors = relation_emb[relation_ids.reshape(-1)].astype(jnp.float32)
        query = complex_product(head_vectors, relation_vectors).astype(jnp.bfloat16)
        query = lax.optimization_barrier(query).astype(jnp.float32)
        positive = lax.optimization_barrier(jnp.sum(query * tail_vectors, axis=1))
        negative = jnp.dot(query, negatives.T, preferred_element_type=jnp.float32)
        largest = jnp.maximum(positive, lax.optimization_barrier(jnp.max(negative, axis=1)))
        pos_exp = jnp.exp(positive - largest)
        neg_exp = jnp.exp(negative - largest[:, None])
        denominator = pos_exp + lax.optimization_barrier(jnp.sum(neg_exp, axis=1))
        pos_grad = (pos_exp / denominator - 1.0) * live_mask
        neg_grad = (neg_exp / denominator[:, None] * live_mask[:, None]).astype(jnp.bfloat16)
        neg_grad = lax.optimization_barrier(neg_grad).astype(jnp.float32)
        query_grad = pos_grad[:, None] * tail_vectors + jnp.dot(neg_grad, negatives, preferred_element_type=jnp.float32)
        tail_part = pos_grad[:, None] * query
        neg_part = jnp.dot(neg_grad.T, query, preferred_element_type=jnp.float32)
        head_grad = jnp.zeros((HROWS, WIDTH), jnp.float32).at[flat_rows].add(conj_product(query_grad, relation_vectors))
        block_grad = jnp.zeros((EB_DEV * TBS, WIDTH), jnp.float32).at[tail_index].add(tail_part).astype(jnp.bfloat16)
        block_grad = lax.optimization_barrier(block_grad).astype(jnp.float32)
        grad_table = grad_table.at[block_ids].add(block_grad.reshape(EB_DEV, TBS, WIDTH))
        head_updated, state_updated = row_adagrad(embedding, adagrad_state, head_grad)
        return ((grad_table, neg_total + neg_part), (head_updated, state_updated))
    initial = (jnp.zeros((TBLOCKS, TBS, WIDTH), jnp.float32), jnp.zeros((NEG, WIDTH), jnp.float32))
    (grad_table, neg_total), (head_updated, state_updated) = lax.scan(one_device, initial, per_device)
    grad_table = grad_table.at[neg_blocks].add(neg_total.reshape(NEGB, TBS, WIDTH))
    tail_updated, tail_state_updated = row_adagrad(tail_emb, tail_state, grad_table)
    return (head_updated.reshape(HEADS, WIDTH), state_updated.reshape(HEADS), tail_updated, tail_state_updated)
```

```python
import jax
import jax.numpy as jnp
from jax import lax
from jax.sharding import PartitionSpec as P

LEARN_RATE = 0.3


def complex_product(left, right):
    half_width = left.shape[-1] // 2
    left_re, left_im = (left[..., :half_width], left[..., half_width:])
    right_re, right_im = (right[..., :half_width], right[..., half_width:])
    return jnp.concatenate(
        [left_re * right_re - left_im * right_im, left_re * right_im + left_im * right_re], axis=-1
    )


def conj_product(left, right):
    half_width = left.shape[-1] // 2
    left_re, left_im = (left[..., :half_width], left[..., half_width:])
    right_re, right_im = (right[..., :half_width], right[..., half_width:])
    return jnp.concatenate(
        [left_re * right_re + left_im * right_im, left_im * right_re - left_re * right_im], axis=-1
    )


def row_adagrad(embedding, adagrad_state, gradient):
    state_next = adagrad_state + jnp.mean(gradient * gradient, axis=-1)
    updated = (
        embedding.astype(jnp.float32) - LEARN_RATE * gradient / jnp.sqrt(state_next)[..., None]
    )
    return (updated.astype(jnp.bfloat16), state_next)


def per_device(
    head_emb,
    head_state,
    tail_emb,
    tail_state,
    relation_emb,
    head_rows,
    relations,
    tail_offsets,
    tail_owner,
    tail_local,
    block_count,
    neg_blocks,
):
    block_total = tail_local.shape[0]
    edge_count = head_rows.shape[1]
    row_width = head_emb.shape[1]
    span_rows = tail_emb.shape[1]
    owned_blocks = tail_emb.shape[0]
    neg_count = neg_blocks.shape[0]
    peer_count = lax.axis_size("tail")
    head_count = lax.axis_size("head")
    tail_rank = lax.axis_index("tail")
    head_rank = lax.axis_index("head")
    piece = span_rows // head_count
    capacity = max(2, (2 * block_total + peer_count - 1) // peer_count)
    owner_rank = tail_owner[:, 0]
    positions = jnp.arange(block_total, dtype=jnp.int32)
    same_owner = owner_rank[:, None] == owner_rank[None, :]
    earlier = positions[None, :] < positions[:, None]
    slot_index = jnp.sum((same_owner & earlier).astype(jnp.int32), axis=1)
    slot_place = owner_rank * capacity + slot_index
    global_block = owner_rank * owned_blocks + tail_local
    slot_ids = (
        jnp.zeros((peer_count * capacity,), jnp.int32)
        .at[slot_place]
        .set(tail_local)
        .reshape(peer_count, capacity)
    )
    incoming_ids = lax.all_to_all(slot_ids, "tail", split_axis=0, concat_axis=0, tiled=True)

    my_rows = lax.dynamic_slice_in_dim(tail_emb, head_rank * piece, piece, axis=1)
    table = lax.all_gather(
        my_rows.reshape(owned_blocks * piece, row_width), ("head", "tail"), axis=0, tiled=True
    )

    def table_row(block, offset):
        return (
            (offset // piece * peer_count + block // owned_blocks) * owned_blocks
            + block % owned_blocks
        ) * piece + offset % piece

    neg_offset = (
        jnp.arange(head_count, dtype=jnp.int32)[:, None, None] * piece
        + jnp.arange(piece, dtype=jnp.int32)[None, None, :]
    )
    neg_index = table_row(neg_blocks[None, :, None], neg_offset).reshape(-1)
    mine_ids = neg_blocks - tail_rank * owned_blocks

    total_edges = block_total * edge_count
    flat_rows = head_rows.reshape(-1)
    block_of = jnp.arange(total_edges, dtype=jnp.int32) // edge_count
    live_rows = (block_of < block_count[0]).astype(jnp.float32)
    tail_index = block_of * span_rows + tail_offsets.reshape(-1)
    vector_index = table_row(global_block[:, None], tail_offsets).reshape(-1)
    relation_vectors = jnp.take(relation_emb, relations.reshape(-1), axis=0)
    head_vectors = jnp.take(head_emb, flat_rows, axis=0)
    query = complex_product(
        head_vectors.astype(jnp.float32), relation_vectors.astype(jnp.float32)
    ).astype(jnp.bfloat16)

    negatives = jnp.take(table, neg_index, axis=0)
    tail_rows = jnp.take(table, vector_index, axis=0)
    query_float = query.astype(jnp.float32)
    positive = jnp.sum(query_float * tail_rows.astype(jnp.float32), axis=1)
    negative = lax.dot_general(
        query, negatives, (((1,), (1,)), ((), ())), preferred_element_type=jnp.float32
    )
    largest = jnp.maximum(positive, jnp.max(negative, axis=1))
    pos_exp = jnp.exp(positive - largest)
    neg_exp = jnp.exp(negative - largest[:, None])
    denominator = pos_exp + jnp.sum(neg_exp, axis=1)
    pos_grad = (pos_exp / denominator - 1.0) * live_rows
    neg_grad = (neg_exp / denominator[:, None] * live_rows[:, None]).astype(jnp.bfloat16)
    tail_part = pos_grad[:, None] * query_float
    block_grad = (
        jnp.zeros((block_total * span_rows, row_width), jnp.float32)
        .at[tail_index]
        .add(tail_part)
        .astype(jnp.bfloat16)
    )
    outgoing = (
        jnp.zeros((peer_count * capacity, span_rows, row_width), jnp.bfloat16)
        .at[slot_place]
        .set(block_grad.reshape(block_total, span_rows, row_width))
    )
    incoming = lax.all_to_all(
        outgoing.reshape(peer_count, capacity, span_rows, row_width),
        "tail",
        split_axis=0,
        concat_axis=0,
        tiled=True,
    )
    neg_part = lax.dot_general(
        neg_grad, query, (((0,), (0,)), ((), ())), preferred_element_type=jnp.float32
    )
    neg_piece = lax.psum_scatter(neg_part, "head", scatter_dimension=0, tiled=True)
    neg_all = lax.psum(neg_piece, "tail").reshape(neg_count, piece, row_width)

    query_grad = pos_grad[:, None] * tail_rows.astype(jnp.float32) + jnp.dot(
        neg_grad, negatives, preferred_element_type=jnp.float32
    )
    head_grad = (
        jnp.zeros(head_emb.shape, jnp.float32)
        .at[flat_rows]
        .add(conj_product(query_grad, relation_vectors.astype(jnp.float32)))
    )
    head_updated, head_state_updated = row_adagrad(head_emb, head_state, head_grad)
    incoming, head_updated = lax.optimization_barrier((incoming, head_updated))

    arrived = incoming.reshape(peer_count * capacity, head_count, piece, row_width)
    arrived_ids = incoming_ids.reshape(-1)
    tail_grad = jnp.stack(
        [
            jnp.sum(
                jnp.where((arrived_ids == b)[:, None, None, None], arrived.astype(jnp.float32), 0.0),
                axis=0,
            )
            for b in range(owned_blocks)
        ],
        axis=1,
    )
    tail_piece = lax.psum_scatter(
        tail_grad.reshape(head_count * owned_blocks * piece, row_width),
        "head",
        scatter_dimension=0,
        tiled=True,
    ).reshape(owned_blocks, piece, row_width)
    own_negs = jnp.stack(
        [
            jnp.sum(jnp.where((mine_ids == b)[:, None, None], neg_all, 0.0), axis=0)
            for b in range(owned_blocks)
        ],
        axis=0,
    )
    state_rows = lax.dynamic_slice_in_dim(tail_state, head_rank * piece, piece, axis=1)
    tail_updated, tail_state_updated = row_adagrad(my_rows, state_rows, tail_piece + own_negs)
    tail_updated = lax.all_gather(
        tail_updated.reshape(owned_blocks * piece, row_width), "head", axis=0, tiled=True
    )
    tail_updated = (
        tail_updated.reshape(head_count, owned_blocks, piece, row_width)
        .transpose(1, 0, 2, 3)
        .reshape(owned_blocks, span_rows, row_width)
    )
    tail_state_updated = (
        lax.all_gather(tail_state_updated, "head", axis=0, tiled=False)
        .transpose(1, 0, 2)
        .reshape(owned_blocks, span_rows)
    )
    return (head_updated, head_state_updated, tail_updated, tail_state_updated)


def solution(mesh):
    placed = (
        P(("head", "tail"), None),
        P(("head", "tail")),
        P("tail", None, None),
        P("tail", None),
        P(),
        P(("head", "tail"), None),
        P(("head", "tail"), None),
        P(("head", "tail"), None),
        P(("head", "tail"), None),
        P(("head", "tail")),
        P(("head", "tail")),
        P(),
    )
    return jax.shard_map(
        per_device,
        mesh=mesh,
        in_specs=placed,
        out_specs=(
            P(("head", "tail"), None),
            P(("head", "tail")),
            P("tail", None, None),
            P("tail", None),
        ),
        check_vma=False,
    )
```
